32 devices in a mesh: tm: 4 (over y, x), freq: 8 (over z, core).
Axes of the slice: x: 2, y: 2, z: 4, core: 2. Of those that a mesh axis runs over, the one named last changes fastest.
Arguments:
- records: bfloat16 [1024, 512, 512], P('freq', 'tm'), may hold values from -4 to 4
- gap_flags: int32 [1024, 16], P('freq', 'tm'), may hold values from -2147483648 to 2147483647
- station_mask: int32 [1024], P('freq'), may hold values 0 or 1
Outputs:
- cross_spectra: float32 [16, 2, 1024, 1024], P('freq', None, 'tm')
The draws below stay inside these ranges and needn't reach their ends.
All inputs are finite; a program needn't handle non-finite values. No bound on the sum of `station_mask` on one device may be relied on, other than what follows from the above.
Results may differ from the reference program's by a relative error of at most 0.0013.
Values may be sent and summed in bfloat16 or wider, within the bound.
No kernel may reach another device: no remote copies, remote signals or barrier semaphores. Data moves between devices by JAX's collectives and lax.ppermute only.
A program may use at most 128 MiB of HBM per device.

```python
import math
import jax
import jax.numpy as jnp
from jax import lax

STATIONS = 1024
SAMPLES = 512
BAND = 16
WINDOWS = 512


def draw_records(key, part):
    key_shared = jax.random.fold_in(key, 12)
    key_ambient = jax.random.fold_in(key, 13)
    key_silent = jax.random.fold_in(key, 14)
    silent = jax.random.uniform(key_silent, (STATIONS, WINDOWS, 1), jnp.float32) < 0.125
    shared = jax.random.normal(key_shared, (1, WINDOWS, SAMPLES), jnp.float32)
    ambient = jax.random.normal(key_ambient, (STATIONS, WINDOWS, SAMPLES), jnp.float32)
    values = 0.5 * shared + 0.866 * ambient
    values = jnp.where(silent, 0.0, values)
    return jnp.clip(values, -4.0, 4.0).astype(jnp.bfloat16)


def draw_gap_flags(key, part):
    key_station = jax.random.fold_in(key, 21)
    key_common = jax.random.fold_in(key, 22)
    station_clear = (jax.random.randint(key_station, (STATIONS, WINDOWS), 0, 20) >= 3).astype(jnp.int32)
    common_clear = (jax.random.randint(key_common, (1, WINDOWS), 0, 20) >= 3).astype(jnp.int32)
    flag_grid = (station_clear * common_clear).reshape(STATIONS, WINDOWS // 32, 32)
    shifts = jnp.arange(32, dtype=jnp.int32)
    return jnp.sum(jnp.left_shift(flag_grid, shifts[None, None, :]), axis=2).astype(jnp.int32)


def touch_ends(values, rng, smallest, high):
    extent = values.shape
    spot = [jax.random.randint(jax.random.fold_in(rng, axis), (), 0, extent[axis]) for axis in range(len(extent))]
    values = values.at[tuple(spot)].set(smallest)
    longest = extent.index(max(extent))
    spot[longest] = (spot[longest] + 1) % extent[longest]
    return values.at[tuple(spot)].set(high)


def setup_inputs(seed: int = 0) -> dict:
    splits = jax.random.split(jax.random.key(seed), 4)
    records = draw_records(jax.random.fold_in(splits[3], 71), 0)
    gap_flags = draw_gap_flags(jax.random.fold_in(splits[3], 71), 0)
    station_mask = touch_ends((jax.random.randint(splits[2], (STATIONS,), 0, 8) < 7).astype(jnp.int32), jax.random.fold_in(splits[2], 1), 0, 1)
    return {"records": records, "gap_flags": gap_flags, "station_mask": station_mask}


FLOOR = 0.25

def transform_table(length, bin_count):
    sample_ids = jnp.arange(length, dtype=jnp.int32)
    bin_ids = jnp.arange(bin_count, dtype=jnp.int32)
    phase_ids = bin_ids[:, None] * sample_ids[None, :] % length
    angles = phase_ids.astype(jnp.float32) * (2.0 * math.pi / length)
    window_taper = 0.5 - 0.5 * jnp.cos(sample_ids.astype(jnp.float32) * (2.0 * math.pi / length))
    factor = window_taper / math.sqrt(length)
    dft_table = jnp.concatenate([jnp.cos(angles) * factor, -jnp.sin(angles) * factor], axis=0)
    return dft_table.astype(jnp.bfloat16)

def unpack_flags(packed_words):
    shifts = jnp.arange(32, dtype=jnp.int32)
    bit_values = jnp.bitwise_and(jnp.right_shift(packed_words[:, :, None], shifts[None, None, :]), 1)
    return bit_values.reshape(packed_words.shape[0], packed_words.shape[1] * 32)

def whiten(records, band_bins):
    bin_count = band_bins + 4
    dft_table = transform_table(records.shape[-1], bin_count)
    spectrum = jnp.einsum('cl,swl->scw', dft_table.astype(jnp.float32), records.astype(jnp.float32), precision=lax.Precision.HIGHEST)
    real_part = spectrum[:, :bin_count]
    imag_part = spectrum[:, bin_count:]
    magnitude = jnp.sqrt(real_part * real_part + imag_part * imag_part)
    smooth = (magnitude[:, 0:band_bins] + magnitude[:, 1:band_bins + 1] + magnitude[:, 2:band_bins + 2] + magnitude[:, 3:band_bins + 3] + magnitude[:, 4:band_bins + 4]) / 5.0
    factor = 1.0 / jnp.maximum(smooth, FLOOR)
    whitened = jnp.stack([real_part[:, 2:band_bins + 2] * factor, imag_part[:, 2:band_bins + 2] * factor], axis=2)
    return whitened.astype(jnp.bfloat16)

def reference(records, gap_flags, station_mask):
    band_bins = BAND
    usable = unpack_flags(gap_flags) * station_mask[:, None]
    group_size = math.gcd(STATIONS, 64)
    grouped = records.reshape(STATIONS // group_size, group_size, WINDOWS, SAMPLES)
    whitened = lax.map(lambda inputs: whiten(inputs, band_bins), grouped)
    whitened = whitened.reshape(STATIONS, band_bins, 2, WINDOWS)
    flag_rows = usable.astype(jnp.bfloat16)
    masked = whitened * flag_rows[:, None, None, :]
    pair_counts = jnp.dot(flag_rows, flag_rows.T, preferred_element_type=jnp.float32)
    divisor = jnp.maximum(pair_counts, 1.0)

    def one_bin(bin_index):
        bin_plane = lax.dynamic_index_in_dim(masked, bin_index, 1, keepdims=False)
        direct = bin_plane.reshape(STATIONS, 2 * WINDOWS)
        turned = jnp.concatenate([bin_plane[:, 1], -bin_plane[:, 0]], axis=1)
        real_part = jnp.dot(direct, direct.T, preferred_element_type=jnp.float32)
        imag_part = jnp.dot(turned, direct.T, preferred_element_type=jnp.float32)
        return jnp.stack([real_part, imag_part]) / divisor
    return lax.map(one_bin, jnp.arange(band_bins, dtype=jnp.int32))
```

```python
import functools
import math

import jax
import jax.numpy as jnp
import numpy as np
from jax import lax
from jax.experimental import pallas as pl
from jax.experimental.pallas import tpu as pltpu
from jax.sharding import PartitionSpec as P

BAND_DEV = 2
FLOOR = 0.25
HALO = 4
STATION_BLOCK = 16


def padded(count):
    return -(-count // 8) * 8


def transform_table(length, bin_count):
    ids = np.arange(length, dtype=np.int64)
    angles = (np.arange(bin_count)[:, None] * ids[None, :] % length) * (2.0 * math.pi / length)
    taper = (0.5 - 0.5 * np.cos(ids * (2.0 * math.pi / length))) / math.sqrt(length)
    table = np.zeros((2 * padded(bin_count), length), np.float32)
    table[:bin_count] = np.cos(angles) * taper
    table[padded(bin_count) : padded(bin_count) + bin_count] = -np.sin(angles) * taper
    return jnp.asarray(table, jnp.bfloat16)


def unpack_flags(packed_words):
    shifts = jnp.arange(32, dtype=jnp.int32)
    bit_values = jnp.bitwise_and(
        jnp.right_shift(packed_words[:, :, None], shifts[None, None, :]), 1
    )
    return bit_values.reshape(packed_words.shape[0], packed_words.shape[1] * 32)


def whiten_kernel(bin_count, table_ref, records_ref, flags_ref, out_ref, spectrum):
    block, windows, length = records_ref.shape
    rows = table_ref.shape[0]
    imag = rows // 2
    bands = bin_count - HALO
    per_device = out_ref.shape[1]
    columns = records_ref[...].reshape(block * windows, length)
    result = lax.dot_general(
        table_ref[...], columns, (((1,), (1,)), ((), ())), preferred_element_type=jnp.float32
    )
    for station in range(block):
        spectrum[station * rows : (station + 1) * rows, :] = result[
            :, station * windows : (station + 1) * windows
        ]
    flags = flags_ref[...]
    real_rows, imag_rows, magnitudes = [], [], []
    for bin_index in range(bin_count):
        real = spectrum[pl.ds(bin_index, block, stride=rows), :]
        turned = spectrum[pl.ds(imag + bin_index, block, stride=rows), :]
        real_rows.append(real)
        imag_rows.append(turned)
        magnitudes.append(jnp.sqrt(real * real + turned * turned))
        if bin_index >= HALO:
            band = bin_index - HALO
            smooth = (
                magnitudes[band]
                + magnitudes[band + 1]
                + magnitudes[band + 2]
                + magnitudes[band + 3]
                + magnitudes[band + 4]
            ) / 5.0
            factor = flags / jnp.maximum(smooth, FLOOR)
            place = (band // per_device, band % per_device)
            out_ref[place[0], place[1], :, :windows] = (real_rows[band + 2] * factor).astype(
                jnp.bfloat16
            )
            out_ref[place[0], place[1], :, windows:] = (imag_rows[band + 2] * factor).astype(
                jnp.bfloat16
            )


def whiten(records, flags, freq_size):
    stations, windows, length = records.shape
    bin_count = BAND_DEV * freq_size + HALO
    table = transform_table(length, bin_count)
    block = STATION_BLOCK
    return pl.pallas_call(
        functools.partial(whiten_kernel, bin_count),
        grid=(stations // block,),
        in_specs=[
            pl.BlockSpec(table.shape, lambda i: (0, 0)),
            pl.BlockSpec((block, windows, length), lambda i: (i, 0, 0)),
            pl.BlockSpec((block, windows), lambda i: (i, 0)),
        ],
        out_specs=pl.BlockSpec((freq_size, BAND_DEV, block, 2 * windows), lambda i: (0, 0, i, 0)),
        out_shape=jax.ShapeDtypeStruct(
            (freq_size, BAND_DEV, stations, 2 * windows), jnp.bfloat16
        ),
        scratch_shapes=[pltpu.VMEM((block * table.shape[0], windows), jnp.float32)],
        cost_estimate=pl.CostEstimate(
            flops=2 * table.shape[0] * records.size,
            bytes_accessed=2 * records.size,
            transcendentals=0,
        ),
        name="whiten",
    )(table, records, flags)


def stack_kernel(layout, chunk_count, place_ref, inverse_ref, *refs):
    spectra = refs[: len(layout)]
    out_ref, held, turned, stage, copy_sems, out_sems = refs[len(layout) :]
    chip = place_ref[0]
    group = place_ref[1]
    _, bins, chunk, depth = held.shape
    width = spectra[0].shape[-1]
    half = width // 2
    copies = {}
    for number, (step, slot, band) in enumerate(layout):
        owner = jnp.bitwise_xor(chip, step)
        lanes = slice(slot * width, (slot + 1) * width)
        target = held.at[owner, :, :, lanes] if band is None else held.at[owner, band, :, lanes]
        copy = pltpu.make_async_copy(spectra[number], target, copy_sems.at[number])
        copy.start()
        copies.setdefault(step, []).append(copy)
    for step in range(chunk_count):
        for copy in copies[step]:
            copy.wait()
    for band in range(bins):
        for start in range(0, depth, width):
            turned[band, :, start : start + half] = held[
                group, band, :, start + half : start + width
            ]
            turned[band, :, start + half : start + width] = -held[
                group, band, :, start : start + half
            ]
    pending = [None, None]
    dims = (((1,), (1,)), ((), ()))
    for step in range(chunk_count):
        owner = jnp.bitwise_xor(chip, step)
        columns = pl.ds(pl.multiple_of(owner * chunk, chunk), chunk)
        inverse = inverse_ref[:, columns]
        for band in range(bins):
            slot = (step * bins + band) % 2
            if pending[slot] is not None:
                pending[slot].wait()
            right = held[owner, band]
            stage[slot, 0] = inverse * lax.dot_general(
                held[group, band], right, dims, preferred_element_type=jnp.float32
            )
            stage[slot, 1] = inverse * lax.dot_general(
                turned[band], right, dims, preferred_element_type=jnp.float32
            )
            pending[slot] = pltpu.make_async_copy(
                stage.at[slot], out_ref.at[band, :, :, columns], out_sems.at[slot]
            )
            pending[slot].start()
    for copy in pending:
        copy.wait()


def stack(spectra, layout, inverse, place, chunk_count, slots):
    chunk, width = spectra[0].shape[-2:]
    rows, stations = inverse.shape
    depth = slots * width
    return pl.pallas_call(
        functools.partial(stack_kernel, layout, chunk_count),
        in_specs=[
            pl.BlockSpec(memory_space=pltpu.SMEM),
            pl.BlockSpec(memory_space=pltpu.VMEM),
        ]
        + [pl.BlockSpec(memory_space=pl.ANY)] * len(spectra),
        out_specs=pl.BlockSpec(memory_space=pl.ANY),
        out_shape=jax.ShapeDtypeStruct((BAND_DEV, 2, rows, stations), jnp.float32),
        scratch_shapes=[
            pltpu.VMEM((chunk_count, BAND_DEV, chunk, depth), jnp.bfloat16),
            pltpu.VMEM((BAND_DEV, chunk, depth), jnp.bfloat16),
            pltpu.VMEM((2, 2, rows, chunk), jnp.float32),
            pltpu.SemaphoreType.DMA((len(layout),)),
            pltpu.SemaphoreType.DMA((2,)),
        ],
        cost_estimate=pl.CostEstimate(
            flops=4 * BAND_DEV * rows * stations * depth,
            bytes_accessed=8 * BAND_DEV * rows * stations,
            transcendentals=0,
        ),
        name="stack",
    )(place, inverse, *spectra)


def swap(value, axis, mask):
    size = lax.axis_size(axis)
    return lax.ppermute(value, axis, [(i, i ^ mask) for i in range(size)])


def in_order(own, other, bit_set, axis):
    return jnp.where(
        bit_set,
        jnp.concatenate([other, own], axis=axis),
        jnp.concatenate([own, other], axis=axis),
    )


def bits_of(size):
    return [1 << b for b in range(size.bit_length() - 1)]


def local(records, gap_flags, station_mask):
    freq_size = lax.axis_size("freq")
    time_size = lax.axis_size("tm")
    freq_index = lax.axis_index("freq")
    time_index = lax.axis_index("tm")
    core = freq_index % 2
    chip = freq_index // 2
    chunk_count = freq_size // 2

    kept_words = gap_flags * station_mask[:, None]
    flags = unpack_flags(kept_words).astype(jnp.float32)
    whitened = whiten(records, flags, freq_size)

    words = kept_words
    for bit in bits_of(freq_size):
        words = in_order(words, swap(words, "freq", bit), (freq_index & bit) != 0, 0)
    for bit in bits_of(time_size):
        words = in_order(words, swap(words, "tm", bit), (time_index & bit) != 0, 1)
    every_flags = unpack_flags(words).astype(jnp.bfloat16)
    stations = every_flags.shape[0]
    rows = stations // time_size
    row_flags = lax.dynamic_slice_in_dim(every_flags, time_index * rows, rows, 0)
    counts = jnp.dot(row_flags, every_flags.T, preferred_element_type=jnp.float32)
    inverse = 1.0 / jnp.maximum(counts, 1.0)

    by_owner = whitened.reshape((chunk_count, 2) + whitened.shape[1:])
    shape = (1, 1) + whitened.shape[1:]

    def part(step, which):
        start = (chip ^ step, which, 0, 0, 0)
        return lax.dynamic_slice(by_owner, start, shape)[0, 0]

    def message(step):
        other = swap(part(step, 1 - core), "freq", 1)
        return in_order(part(step, core), other, core == 1, 1)

    chunks = [message(step) for step in range(chunk_count)]
    chunks = [chunks[0]] + [swap(chunks[step], "freq", 2 * step) for step in range(1, chunk_count)]

    spectra, layout = [], []
    time_bits = bits_of(time_size)
    for step, chunk in enumerate(chunks):
        blocks = {0: [chunk[b] for b in range(BAND_DEV)]}
        spectra.append(chunk)
        layout.append((step, 0, None))
        for mask in sorted(range(1, time_size), key=lambda m: bin(m).count("1")):
            inside = [bit for bit in time_bits if mask & bit]
            if len(inside) == 1:
                arrived = swap(chunk, "tm", mask)
                blocks[mask] = [arrived[b] for b in range(BAND_DEV)]
                spectra.append(arrived)
                layout.append((step, mask, None))
            else:
                blocks[mask] = []
                for b in range(BAND_DEV):
                    bit = inside[b % len(inside)]
                    arrived = swap(blocks[mask ^ bit][b], "tm", bit)
                    blocks[mask].append(arrived)
                    spectra.append(arrived)
                    layout.append((step, mask, b))

    place = jnp.stack([chip, time_index]).astype(jnp.int32)
    return stack(spectra, layout, inverse, place, chunk_count, time_size)


def solution(mesh):
    placed = (P("freq", "tm", None), P("freq", "tm"), P("freq"))
    return jax.shard_map(
        local, mesh=mesh, in_specs=placed, out_specs=P("freq", None, "tm", None), check_vma=False
    )
```
